512 devices in a mesh: mode: 2 (over core), oth: 256 (over z, y, x).
Axes of the slice: x: 4, y: 8, z: 8, core: 2. Of those that a mesh axis runs over, the one named last changes fastest.
Arguments:
- tensor: float32 [512, 4, 262144], P('mode', None, 'oth'), may hold values from -20 to 20
- start_basis: float32 [512, 128], replicated, may hold values from -6 to 6
Outputs:
- core_slab: float32 [128, 4, 262144], P('mode', None, 'oth')
- triangle: float32 [512, 512], replicated
The draws below stay inside these ranges and needn't reach their ends.
All inputs are finite; a program needn't handle non-finite values.
Results may differ from the reference program's by a relative error of at most 0.0003.
Values sent between devices are 32-bit elements; how exact they have to be, the bound alone decides.
A program may use at most 64 MiB of HBM per device.

```python
import math
import jax
import jax.numpy as jnp
from jax import lax

N1 = 512
RANK = 128
N4 = 4
ITERS = 3
YZ = 262144


shared_count = 8


def draw_tensor(key, part):
    keys = jax.random.split(jax.random.fold_in(key, 11), 7)
    row_scale = jnp.exp(jax.random.uniform(keys[0], (N1, 1, 1), jnp.float32, math.log(0.3), math.log(3.0)))
    coupling = jax.random.uniform(keys[4], (N1 - 1, 1, 1), jnp.float32, 0.3, 0.6)
    loadings = jax.random.uniform(keys[5], (shared_count, N1, 1, 1), jnp.float32, -0.2, 0.2)
    noise = jnp.clip(jax.random.normal(keys[1], (N1, N4, YZ), jnp.float32), -6.0, 6.0)
    components = jnp.clip(jax.random.normal(keys[6], (shared_count, N4, YZ), jnp.float32), -6.0, 6.0)
    below = jnp.concatenate([jnp.zeros((1, N4, YZ), jnp.float32), coupling * noise[:-1]], axis=0)
    mixed = noise + below
    for index in range(shared_count):
        mixed = mixed + loadings[index] * components[index][None, :, :]
    values = row_scale * mixed
    return jnp.clip(values, -20.0, 20.0)


def centred(rng, shape, deviation, limit, dtype=jnp.bfloat16):
    array = deviation * jax.random.normal(rng, shape, jnp.float32)
    return jnp.clip(array, min=-limit, max=limit).astype(dtype)


def setup_inputs(seed: int = 0) -> dict:
    key_list = jax.random.split(jax.random.key(seed), 3)
    tensor = draw_tensor(jax.random.fold_in(key_list[2], 71), 0)
    start_basis = centred(key_list[1], (N1, RANK), 1.0, 6.0, jnp.float32)
    return dict(tensor=tensor, start_basis=start_basis)


def subspace(triangle, start_basis):
    basis = start_basis
    for sweep in range(ITERS):
        reduced = jnp.dot(triangle.T.astype(jnp.float32), basis.astype(jnp.float32), precision=lax.Precision.HIGHEST, preferred_element_type=jnp.float32)
        images = jnp.dot(triangle.astype(jnp.float32), reduced.astype(jnp.float32), precision=lax.Precision.HIGHEST, preferred_element_type=jnp.float32)
        gram_small = jnp.dot(images.T.astype(jnp.float32), images.astype(jnp.float32), precision=lax.Precision.HIGHEST, preferred_element_type=jnp.float32)
        factor_lower = jnp.linalg.cholesky(gram_small)
        basis = lax.linalg.triangular_solve(factor_lower, images, left_side=False, lower=True, transpose_a=True)
    return basis

def reference(tensor, start_basis):
    unfolded = tensor.reshape(N1, N4 * YZ)
    covariance = jnp.dot(unfolded.astype(jnp.float32), unfolded.T.astype(jnp.float32), precision=lax.Precision.HIGHEST, preferred_element_type=jnp.float32) / (N4 * YZ)
    triangle = jnp.linalg.cholesky(covariance)
    basis = subspace(triangle, start_basis)
    core_slab = jnp.dot(basis.T.astype(jnp.float32), unfolded.astype(jnp.float32), precision=lax.Precision.HIGHEST, preferred_element_type=jnp.float32)
    return (core_slab.reshape(RANK, N4, YZ), triangle)
```

```python
import jax
import jax.numpy as jnp
from jax import lax
from jax.experimental import pallas as pl
from jax.experimental.pallas import tpu as pltpu
from jax.sharding import PartitionSpec as P

ITERS = 3
T = 128
XS, YS, ZS = 4, 8, 8
HIGH = lax.Precision.HIGHEST


def sum_kernel(diag, cross, out, work, half_in, in1, in2, in3, send_sem, recv_sem):
    mode = lax.axis_index("mode")
    oth = lax.axis_index("oth")
    x = lax.rem(oth, XS)
    y = lax.rem(oth // XS, YS)
    z = oth // (XS * YS)
    rows = work.shape[0]
    part = rows // 2
    piece = part // ZS
    own = cross.shape[0] // 2
    base = rows - own
    other = {"mode": 1 - mode, "oth": oth}

    def along(axis, place):
        if axis == "z":
            cell = place * (XS * YS) + y * XS + x
        elif axis == "y":
            cell = z * (XS * YS) + place * XS + x
        else:
            cell = z * (XS * YS) + y * XS + place
        return {"mode": mode, "oth": cell}

    size = {"x": XS, "y": YS, "z": ZS}
    here = {"x": x, "y": y, "z": z}

    def peer(axis, step):
        return lax.rem(here[axis] + step, size[axis])

    barrier = pltpu.get_barrier_semaphore()
    pl.semaphore_signal(barrier, inc=1, device_id=other)
    count = 1
    for axis in "zyx":
        for step in range(1, size[axis]):
            pl.semaphore_signal(barrier, inc=1, device_id=along(axis, peer(axis, step)))
            count += 1
    pl.semaphore_wait(barrier, count)

    def copy(src, dst, slot, device):
        return pltpu.make_async_remote_copy(
            src_ref=src,
            dst_ref=dst,
            send_sem=send_sem.at[slot],
            recv_sem=recv_sem.at[slot],
            device_id=device,
        )

    pending = []
    first = copy(
        cross.at[pl.ds(pl.multiple_of((1 - mode) * own, 8), own)], half_in, 0, other
    )
    first.start()
    work[:base] = diag[...]
    first.wait_recv()
    work[base:] = cross[pl.ds(pl.multiple_of(mode * own, 8), own)] + half_in[...]
    pending.append(first)

    plans = (("z", "y"), ("y", "z"))
    slot = 1
    stage = []
    for index, (major, minor) in enumerate(plans):
        for step in range(1, size[major]):
            to = peer(major, step)
            start = pl.multiple_of(index * part + to * piece, 8)
            item = copy(
                work.at[pl.ds(start, piece)], in1.at[index, here[major]], slot, along(major, to)
            )
            item.start()
            stage.append(item)
            slot += 1
    for index, (major, minor) in enumerate(plans):
        start = pl.multiple_of(index * part + here[major] * piece, 8)
        in1[index, here[major]] = work[pl.ds(start, piece)]
    position = 0
    second = []
    for index, (major, minor) in enumerate(plans):
        for step in range(1, size[major]):
            stage[position].wait_recv()
            position += 1
        total = in1[index, 0]
        for place in range(1, size[major]):
            total = total + in1[index, place]
        in2[index, here[minor]] = total
        for step in range(1, size[minor]):
            spot = in2.at[index, here[minor]]
            item = copy(spot, spot, slot, along(minor, peer(minor, step)))
            item.start()
            second.append(item)
            slot += 1
    pending += stage
    position = 0
    third = []
    for index, (major, minor) in enumerate(plans):
        for step in range(1, size[minor]):
            second[position].wait_recv()
            position += 1
        total = in2[index, 0]
        for place in range(1, size[minor]):
            total = total + in2[index, place]
        in3[index, x] = total
        for step in range(1, XS):
            spot = in3.at[index, x]
            item = copy(spot, spot, slot, along("x", peer("x", step)))
            item.start()
            third.append(item)
            slot += 1
    pending += second
    position = 0
    fourth = []
    passed = []
    for index, (major, minor) in enumerate(plans):
        for step in range(1, XS):
            third[position].wait_recv()
            position += 1
        total = in3[index, 0]
        for place in range(1, XS):
            total = total + in3[index, place]
        start = pl.multiple_of(index * part + here[major] * piece, 8)
        out[mode, pl.ds(start, piece)] = total
        spot = out.at[mode, pl.ds(start, piece)]
        for step in range(1, size[major]):
            item = copy(spot, spot, slot, along(major, peer(major, step)))
            item.start()
            fourth.append(item)
            slot += 1
        item = copy(spot, spot, slot, other)
        item.start()
        passed.append(item)
        slot += 1
    pending += third
    position = 0
    for index, (major, minor) in enumerate(plans):
        for step in range(1, size[major]):
            fourth[position].wait_recv()
            position += 1
            source = lax.rem(here[major] + (size[major] - step), size[major])
            start = pl.multiple_of(index * part + source * piece, 8)
            spot = out.at[mode, pl.ds(start, piece)]
            item = copy(spot, spot, slot, other)
            item.start()
            passed.append(item)
            slot += 1
    pending += fourth
    for item in passed:
        item.wait_recv()
    pending += passed
    for item in pending:
        item.wait_send()


def summed(diag, cross):
    rows = diag.shape[0] + cross.shape[0] // 2
    piece = rows // 2 // ZS
    copies = 1 + 14 + 14 + 6 + 14 + 2 + 14
    return pl.pallas_call(
        sum_kernel,
        out_shape=jax.ShapeDtypeStruct((2, rows, T), jnp.float32),
        in_specs=[pl.BlockSpec(memory_space=pltpu.VMEM)] * 2,
        out_specs=pl.BlockSpec(memory_space=pltpu.VMEM),
        scratch_shapes=[
            pltpu.VMEM((rows, T), jnp.float32),
            pltpu.VMEM((cross.shape[0] // 2, T), jnp.float32),
            pltpu.VMEM((2, ZS, piece, T), jnp.float32),
            pltpu.VMEM((2, ZS, piece, T), jnp.float32),
            pltpu.VMEM((2, XS, piece, T), jnp.float32),
            pltpu.SemaphoreType.DMA((copies,)),
            pltpu.SemaphoreType.DMA((copies,)),
        ],
        compiler_params=pltpu.CompilerParams(collective_id=0, has_side_effects=True),
        name="covariance_sum",
    )(diag, cross)


def dot(a, b, ca, cb):
    return lax.dot_general(
        a, b, (((ca,), (cb,)), ((), ())), precision=HIGH, preferred_element_type=jnp.float32
    )


def factor(mats, uppers):
    groups = T // 8
    lane = lax.broadcasted_iota(jnp.int32, (8, T), 1)
    sub = lax.broadcasted_iota(jnp.int32, (8, T), 0)

    def body(k, state):
        new_state = []
        for mat, upper in zip(state, uppers):
            mat = list(mat)
            done = jnp.zeros((8, T), jnp.float32)
            for i in range(8):
                row = jnp.broadcast_to(mat[0][i : i + 1, :], (8, T))
                pivot = jnp.broadcast_to(row[:, i : i + 1], (8, T))
                inv = lax.rsqrt(pivot)
                at = lane == i
                row_one = jnp.where(at, 1.0, row)
                scaled = row_one * (inv * inv)
                done = jnp.where(sub == i, row * inv, done)
                for g in range(groups):
                    col = jnp.broadcast_to(mat[g][:, i : i + 1], (8, T))
                    if g == 0:
                        col = jnp.where(sub > i, col, 0.0)
                    else:
                        col = jnp.where(g + k < groups, col, 0.0)
                    mat[g] = jnp.where(at, 0.0, mat[g]) - col * scaled
                mat[0] = jnp.where(sub == i, row_one * inv, mat[0])
            upper[pl.ds(pl.multiple_of(k * 8, 8), 8), :] = pltpu.roll(done, k * 8, axis=1)
            mat = [pltpu.roll(m, T - 8, axis=1) for m in mat]
            new_state.append(tuple(mat[1:] + mat[:1]))
        return tuple(new_state)

    state = tuple(tuple(m[8 * g : 8 * g + 8, :] for g in range(groups)) for m in mats)
    state = lax.fori_loop(0, groups, body, state)
    row = lax.broadcasted_iota(jnp.int32, (T, T), 0)
    col = lax.broadcasted_iota(jnp.int32, (T, T), 1)
    inverses = [jnp.where(row >= col, jnp.concatenate(s, axis=0), 0.0) for s in state]
    lowers = [jnp.where(row <= col, u[...], 0.0).T for u in uppers]
    return lowers, inverses


PLACES = (((0, 0), (1, 0), (1, 1), (2, 0), (2, 1)), ((2, 2), (3, 2), (3, 3), (3, 0), (3, 1)))


def small_kernel(scale, sums, start, triangle, basis_out, covar, work, images, upper1, upper2):
    blocks = covar.shape[0] // T
    for m in range(2):
        for b, (r, c) in enumerate(PLACES[m]):
            block = sums[m, b] * scale
            covar[r * T : r * T + T, c * T : c * T + T] = block
            work[r * T : r * T + T, c * T : c * T + T] = block
            if r != c:
                covar[c * T : c * T + T, r * T : r * T + T] = block.T
    basis_out[...] = start[...]
    for r in range(blocks):
        lo = r * T
        mats = [work[lo : lo + T, lo : lo + T]]
        uppers = [upper1]
        if r < ITERS:
            images[...] = dot(covar[...], basis_out[...], 1, 0)
            mats.append(dot(images[...], images[...], 0, 0))
            uppers.append(upper2)
        lowers, inverses = factor(mats, uppers)
        triangle[lo : lo + T, lo : lo + T] = lowers[0]
        if r < ITERS:
            basis_out[...] = dot(images[...], inverses[1], 1, 1)
        if r > 0:
            triangle[:lo, lo : lo + T] = jnp.zeros((lo, T), jnp.float32)
        if r < blocks - 1:
            panel = dot(work[lo + T :, lo : lo + T], inverses[0], 1, 1)
            triangle[lo + T :, lo : lo + T] = panel
            for c in range(r + 1, blocks):
                top = c * T
                work[top:, top : top + T] = work[top:, top : top + T] - dot(
                    panel[top - lo - T :, :], panel[top - lo - T : top - lo, :], 1, 1
                )


def small(scale, sums, start_basis):
    n, rank = start_basis.shape
    return pl.pallas_call(
        lambda *refs: small_kernel(scale, *refs),
        out_shape=[
            jax.ShapeDtypeStruct((n, n), jnp.float32),
            jax.ShapeDtypeStruct((n, rank), jnp.float32),
        ],
        in_specs=[pl.BlockSpec(memory_space=pltpu.VMEM)] * 2,
        out_specs=[pl.BlockSpec(memory_space=pltpu.VMEM)] * 2,
        scratch_shapes=[
            pltpu.VMEM((n, n), jnp.float32),
            pltpu.VMEM((n, n), jnp.float32),
            pltpu.VMEM((n, rank), jnp.float32),
            pltpu.VMEM((T, T), jnp.float32),
            pltpu.VMEM((T, T), jnp.float32),
        ],
        name="factors",
    )(sums, start_basis)


def local(tensor, start_basis):
    rows, components, cells = tensor.shape
    total = components * cells * lax.axis_size("oth")
    mode = lax.axis_index("mode")
    swap = [(0, 1), (1, 0)]
    half = cells // 2
    away = lax.dynamic_slice_in_dim(tensor, (1 - mode) * half, half, 2)
    kept = lax.dynamic_slice_in_dim(tensor, mode * half, half, 2)
    arrived = lax.ppermute(away, "mode", swap)
    both = (((1, 2), (1, 2)), ((), ()))
    own = lax.dot_general(tensor, tensor, both, precision=HIGH, preferred_element_type=jnp.float32)
    mixed = lax.dot_general(kept, arrived, both, precision=HIGH, preferred_element_type=jnp.float32)
    mixed = jnp.where(mode == 0, mixed.T, mixed)
    diag = jnp.concatenate([own[:T, :T], own[T:, :T], own[T:, T:]], axis=0)
    cross = jnp.concatenate([mixed[:T, :T], mixed[:T, T:], mixed[T:, :T], mixed[T:, T:]], axis=0)
    sums = summed(diag, cross).reshape(2, -1, T, T)
    triangle, basis = small(1.0 / total, sums, start_basis)
    rank = basis.shape[1] // 2
    own_rows = lax.dynamic_slice_in_dim(basis, mode * rows, rows, 0)
    given = lax.dynamic_slice_in_dim(own_rows, (1 - mode) * rank, rank, 1)
    mine = lax.dynamic_slice_in_dim(own_rows, mode * rank, rank, 1)
    first = (((0,), (0,)), ((), ()))
    sent = lax.ppermute(
        lax.dot_general(given, tensor, first, precision=HIGH, preferred_element_type=jnp.float32),
        "mode",
        swap,
    )
    stays = lax.dot_general(mine, tensor, first, precision=HIGH, preferred_element_type=jnp.float32)
    return (stays + sent, triangle)


def solution(mesh):
    return jax.shard_map(
        local,
        mesh=mesh,
        in_specs=(P("mode", None, "oth"), P()),
        out_specs=(P("mode", None, "oth"), P()),
        check_vma=False,
    )
```

```python
import jax
import jax.numpy as jnp
from jax import lax
from jax.experimental import pallas as pl
from jax.experimental.pallas import tpu as pltpu
from jax.sharding import PartitionSpec as P

ITERS = 3
T = 128
XS, YS, ZS = 4, 8, 8
HIGH = lax.Precision.HIGHEST


def sum_kernel(diag, cross, out, work, half_in, in1, in2, in3, send_sem, recv_sem):
    mode = lax.axis_index("mode")
    oth = lax.axis_index("oth")
    x = lax.rem(oth, XS)
    y = lax.rem(oth // XS, YS)
    z = oth // (XS * YS)
    rows = work.shape[0]
    part = rows // 2
    piece = part // ZS
    own = cross.shape[0] // 2
    base = rows - own
    other = {"mode": 1 - mode, "oth": oth}

    def along(axis, place):
        if axis == "z":
            cell = place * (XS * YS) + y * XS + x
        elif axis == "y":
            cell = z * (XS * YS) + place * XS + x
        else:
            cell = z * (XS * YS) + y * XS + place
        return {"mode": mode, "oth": cell}

    size = {"x": XS, "y": YS, "z": ZS}
    here = {"x": x, "y": y, "z": z}

    def peer(axis, step):
        return lax.rem(here[axis] + step, size[axis])

    barrier = pltpu.get_barrier_semaphore()
    pl.semaphore_signal(barrier, inc=1, device_id=other)
    count = 1
    for axis in "zyx":
        for step in range(1, size[axis]):
            pl.semaphore_signal(barrier, inc=1, device_id=along(axis, peer(axis, step)))
            count += 1
    pl.semaphore_wait(barrier, count)

    def copy(src, dst, slot, device):
        return pltpu.make_async_remote_copy(
            src_ref=src,
            dst_ref=dst,
            send_sem=send_sem.at[slot],
            recv_sem=recv_sem.at[slot],
            device_id=device,
        )

    pending = []
    first = copy(
        cross.at[pl.ds(pl.multiple_of((1 - mode) * own, 8), own)], half_in, 0, other
    )
    first.start()
    work[:base] = diag[...]
    first.wait_recv()
    work[base:] = cross[pl.ds(pl.multiple_of(mode * own, 8), own)] + half_in[...]
    pending.append(first)

    plans = (("z", "y"), ("y", "z"))
    slot = 1
    stage = []
    for index, (major, minor) in enumerate(plans):
        for step in range(1, size[major]):
            to = peer(major, step)
            start = pl.multiple_of(index * part + to * piece, 8)
            item = copy(
                work.at[pl.ds(start, piece)], in1.at[index, here[major]], slot, along(major, to)
            )
            item.start()
            stage.append(item)
            slot += 1
    for index, (major, minor) in enumerate(plans):
        start = pl.multiple_of(index * part + here[major] * piece, 8)
        in1[index, here[major]] = work[pl.ds(start, piece)]
    position = 0
    second = []
    for index, (major, minor) in enumerate(plans):
        for step in range(1, size[major]):
            stage[position].wait_recv()
            position += 1
        total = in1[index, 0]
        for place in range(1, size[major]):
            total = total + in1[index, place]
        in2[index, here[minor]] = total
        for step in range(1, size[minor]):
            spot = in2.at[index, here[minor]]
            item = copy(spot, spot, slot, along(minor, peer(minor, step)))
            item.start()
            second.append(item)
            slot += 1
    pending += stage
    position = 0
    third = []
    for index, (major, minor) in enumerate(plans):
        for step in range(1, size[minor]):
            second[position].wait_recv()
            position += 1
        total = in2[index, 0]
        for place in range(1, size[minor]):
            total = total + in2[index, place]
        in3[index, x] = total
        for step in range(1, XS):
            spot = in3.at[index, x]
            item = copy(spot, spot, slot, along("x", peer("x", step)))
            item.start()
            third.append(item)
            slot += 1
    pending += second
    position = 0
    fourth = []
    passed = []
    for index, (major, minor) in enumerate(plans):
        for step in range(1, XS):
            third[position].wait_recv()
            position += 1
        total = in3[index, 0]
        for place in range(1, XS):
            total = total + in3[index, place]
        start = pl.multiple_of(index * part + here[major] * piece, 8)
        out[mode, pl.ds(start, piece)] = total
        spot = out.at[mode, pl.ds(start, piece)]
        for step in range(1, size[major]):
            item = copy(spot, spot, slot, along(major, peer(major, step)))
            item.start()
            fourth.append(item)
            slot += 1
        item = copy(spot, spot, slot, other)
        item.start()
        passed.append(item)
        slot += 1
    pending += third
    position = 0
    for index, (major, minor) in enumerate(plans):
        for step in range(1, size[major]):
            fourth[position].wait_recv()
            position += 1
            source = lax.rem(here[major] + (size[major] - step), size[major])
            start = pl.multiple_of(index * part + source * piece, 8)
            spot = out.at[mode, pl.ds(start, piece)]
            item = copy(spot, spot, slot, other)
            item.start()
            passed.append(item)
            slot += 1
    pending += fourth
    for item in passed:
        item.wait_recv()
    pending += passed
    for item in pending:
        item.wait_send()


def summed(diag, cross):
    rows = diag.shape[0] + cross.shape[0] // 2
    piece = rows // 2 // ZS
    copies = 1 + 14 + 14 + 6 + 14 + 2 + 14
    return pl.pallas_call(
        sum_kernel,
        out_shape=jax.ShapeDtypeStruct((2, rows, T), jnp.float32),
        in_specs=[pl.BlockSpec(memory_space=pltpu.VMEM)] * 2,
        out_specs=pl.BlockSpec(memory_space=pltpu.VMEM),
        scratch_shapes=[
            pltpu.VMEM((rows, T), jnp.float32),
            pltpu.VMEM((cross.shape[0] // 2, T), jnp.float32),
            pltpu.VMEM((2, ZS, piece, T), jnp.float32),
            pltpu.VMEM((2, ZS, piece, T), jnp.float32),
            pltpu.VMEM((2, XS, piece, T), jnp.float32),
            pltpu.SemaphoreType.DMA((copies,)),
            pltpu.SemaphoreType.DMA((copies,)),
        ],
        compiler_params=pltpu.CompilerParams(collective_id=0, has_side_effects=True),
        name="covariance_sum",
    )(diag, cross)


def dot(a, b, ca, cb):
    return lax.dot_general(
        a, b, (((ca,), (cb,)), ((), ())), precision=HIGH, preferred_element_type=jnp.float32
    )


def thirds(x):
    high = x.astype(jnp.bfloat16).astype(jnp.float32)
    rest = x - high
    middle = rest.astype(jnp.bfloat16).astype(jnp.float32)
    return high, middle, rest - middle


def outer(a, b):
    ah, am, al = thirds(a)
    bh, bm, bl = thirds(b)
    left = jnp.concatenate([ah, ah, am, am, ah, al], axis=0).astype(jnp.bfloat16)
    right = jnp.concatenate([bh, bm, bh, bm, bl, bh], axis=0).astype(jnp.bfloat16)
    return lax.dot_general(
        left, right, (((0,), (0,)), ((), ())), preferred_element_type=jnp.float32
    )


def factor(mats, uppers):
    groups = T // 8
    lane = lax.broadcasted_iota(jnp.int32, (8, T), 1)
    sub = lax.broadcasted_iota(jnp.int32, (8, T), 0)

    def spread(v, i):
        return jnp.broadcast_to(v[i : i + 1, :], (8, T))

    def column(v, i):
        return jnp.broadcast_to(v[:, i : i + 1], (8, T))

    def body(k, state):
        new_state = []
        keep = lane < jnp.where(k == 0, T, T - 8)
        more = k < groups - 1
        active = (lane >= 8) & (lane < T - 8 * k)
        for (mat, left, right), upper in zip(state, uppers):
            mat = list(mat)
            late = outer(left, right)
            for g in range(1, groups - 1):
                mat[g] = jnp.where(keep, mat[g], 0.0) - late[8 * g : 8 * g + 8, :]
            head, following = mat[0], mat[1]
            heads = [column(head, i) for i in range(8)]
            nexts = [jnp.where(more, column(following, i), 0.0) for i in range(8)]
            done = jnp.zeros((8, T), jnp.float32)
            for i in range(8):
                row = spread(head, i)
                inv = lax.rsqrt(spread(heads[i], i))
                square = inv * inv
                at = lane == i
                row_one = jnp.where(at, 1.0, row)
                scaled = row_one * square
                done = jnp.where(sub == i, row * inv, done)
                below = jnp.where(sub > i, heads[i], 0.0)
                for j in range(i + 1, 8):
                    factor_j = spread(heads[j], i) * square
                    heads[j] = heads[j] - below * factor_j
                    nexts[j] = nexts[j] - nexts[i] * factor_j
                head = jnp.where(at, 0.0, head) - below * scaled
                head = jnp.where(sub == i, row_one * inv, head)
                following = jnp.where(at, 0.0, following) - nexts[i] * scaled
            upper[pl.ds(pl.multiple_of(k * 8, 8), 8), :] = pltpu.roll(done, k * 8, axis=1)
            left = jnp.where(active, head, 0.0)
            right = jnp.where((lane < 8) & (lane > sub), 0.0, head)
            mat = [head, following] + mat[2:]
            mat = [pltpu.roll(m, T - 8, axis=1) for m in mat]
            left = pltpu.roll(left, T - 8, axis=1)
            right = pltpu.roll(right, T - 8, axis=1)
            new_state.append((tuple(mat[1:] + mat[:1]), left, right))
        return tuple(new_state)

    zero = jnp.zeros((8, T), jnp.float32)
    state = tuple(
        (tuple(m[8 * g : 8 * g + 8, :] for g in range(groups)), zero, zero) for m in mats
    )
    state = lax.fori_loop(0, groups, body, state)
    row = lax.broadcasted_iota(jnp.int32, (T, T), 0)
    col = lax.broadcasted_iota(jnp.int32, (T, T), 1)
    inverses = [jnp.where(row >= col, jnp.concatenate(s[0], axis=0), 0.0) for s in state]
    lowers = [jnp.where(row <= col, u[...], 0.0).T for u in uppers]
    return lowers, inverses


PLACES = (((0, 0), (1, 0), (1, 1), (2, 0), (2, 1)), ((2, 2), (3, 2), (3, 3), (3, 0), (3, 1)))


def small_kernel(
    scale, sums, start, triangle, basis_turned, covar, work, images, basis, upper1, upper2
):
    blocks = covar.shape[0] // T
    for m in range(2):
        for b, (r, c) in enumerate(PLACES[m]):
            block = sums[m, b] * scale
            covar[r * T : r * T + T, c * T : c * T + T] = block
            work[r * T : r * T + T, c * T : c * T + T] = block
            if r != c:
                covar[c * T : c * T + T, r * T : r * T + T] = block.T
    basis[...] = start[...]
    for r in range(blocks):
        lo = r * T
        mats = [work[lo : lo + T, lo : lo + T]]
        uppers = [upper1]
        if r < ITERS:
            images[...] = dot(covar[...], basis[...], 1, 0)
            mats.append(dot(images[...], images[...], 0, 0))
            uppers.append(upper2)
        lowers, inverses = factor(mats, uppers)
        triangle[lo : lo + T, lo : lo + T] = lowers[0]
        if r < ITERS - 1:
            basis[...] = dot(images[...], inverses[1], 1, 1)
        elif r == ITERS - 1:
            basis_turned[...] = dot(inverses[1], images[...], 1, 1)
        if r > 0:
            triangle[:lo, lo : lo + T] = jnp.zeros((lo, T), jnp.float32)
        if r < blocks - 1:
            panel = dot(work[lo + T :, lo : lo + T], inverses[0], 1, 1)
            triangle[lo + T :, lo : lo + T] = panel
            for c in range(r + 1, blocks):
                top = c * T
                work[top:, top : top + T] = work[top:, top : top + T] - dot(
                    panel[top - lo - T :, :], panel[top - lo - T : top - lo, :], 1, 1
                )


def small(scale, sums, start_basis):
    n, rank = start_basis.shape
    return pl.pallas_call(
        lambda *refs: small_kernel(scale, *refs),
        out_shape=[
            jax.ShapeDtypeStruct((n, n), jnp.float32),
            jax.ShapeDtypeStruct((rank, n), jnp.float32),
        ],
        in_specs=[pl.BlockSpec(memory_space=pltpu.VMEM)] * 2,
        out_specs=[pl.BlockSpec(memory_space=pltpu.VMEM)] * 2,
        scratch_shapes=[
            pltpu.VMEM((n, n), jnp.float32),
            pltpu.VMEM((n, n), jnp.float32),
            pltpu.VMEM((n, rank), jnp.float32),
            pltpu.VMEM((n, rank), jnp.float32),
            pltpu.VMEM((T, T), jnp.float32),
            pltpu.VMEM((T, T), jnp.float32),
        ],
        name="factors",
    )(sums, start_basis)


def partner():
    mode = lax.axis_index("mode")
    return mode, {"mode": 1 - mode, "oth": lax.axis_index("oth")}


def greet(other):
    barrier = pltpu.get_barrier_semaphore()
    pl.semaphore_signal(barrier, inc=1, device_id=other)
    pl.semaphore_wait(barrier, 1)


def pair_kernel(
    tensor, diag, cross, arrived, whole, got, square, mixed, load_sem, send_sem, recv_sem, store_sem
):
    mode, other = partner()
    fields, rows, cells = whole.shape
    half = cells // 2
    kept = pl.ds(pl.multiple_of(mode * half, T), half)
    away = pl.ds(pl.multiple_of((1 - mode) * half, T), half)

    def load(c):
        return pltpu.make_async_copy(tensor.at[:, c, :], whole.at[c], load_sem.at[c])

    def send(c):
        return pltpu.make_async_remote_copy(
            src_ref=whole.at[c, :, away],
            dst_ref=got.at[c],
            send_sem=send_sem.at[c],
            recv_sem=recv_sem.at[c],
            device_id=other,
        )

    def store(c):
        return pltpu.make_async_copy(got.at[c], arrived.at[c], store_sem.at[c])

    for c in range(fields):
        load(c).start()
    greet(other)
    for c in range(fields):
        load(c).wait()
        send(c).start()
    square[...] = jnp.zeros_like(square)
    mixed[...] = jnp.zeros_like(mixed)

    @pl.loop(0, fields)
    def _(c):
        square[...] += dot(whole[c], whole[c], 1, 1)

    @pl.loop(0, fields)
    def _(c):
        send(c).wait_recv()
        store(c).start()
        mixed[...] += dot(whole[c, :, kept], got[c], 1, 1)

    diag[:T] = square[:T, :T]
    diag[T : 2 * T] = square[T:, :T]
    diag[2 * T :] = square[T:, T:]
    lower = jnp.where(mode == 0, mixed[...].T, mixed[...])
    cross[:T] = lower[:T, :T]
    cross[T : 2 * T] = lower[:T, T:]
    cross[2 * T : 3 * T] = lower[T:, :T]
    cross[3 * T :] = lower[T:, T:]
    for c in range(fields):
        store(c).wait()
        send(c).wait_send()


def pair(tensor):
    rows, fields, cells = tensor.shape
    any_spec = pl.BlockSpec(memory_space=pl.ANY)
    vmem = pl.BlockSpec(memory_space=pltpu.VMEM)
    return pl.pallas_call(
        pair_kernel,
        out_shape=[
            jax.ShapeDtypeStruct((3 * T, T), jnp.float32),
            jax.ShapeDtypeStruct((4 * T, T), jnp.float32),
            jax.ShapeDtypeStruct((fields, rows, cells // 2), jnp.float32),
        ],
        in_specs=[any_spec],
        out_specs=[vmem, vmem, any_spec],
        scratch_shapes=[
            pltpu.VMEM((fields, rows, cells), jnp.float32),
            pltpu.VMEM((fields, rows, cells // 2), jnp.float32),
            pltpu.VMEM((rows, rows), jnp.float32),
            pltpu.VMEM((rows, rows), jnp.float32),
        ]
        + [pltpu.SemaphoreType.DMA((fields,))] * 4,
        compiler_params=pltpu.CompilerParams(collective_id=1, has_side_effects=True),
        name="covariance_terms",
    )(tensor)


def project_kernel(
    basis, tensor, arrived, out, own, theirs, slab, own_sem, their_sem, send_sem, recv_sem, store_sem
):
    mode, other = partner()
    fields, rows, half = own.shape
    kept = pl.ds(pl.multiple_of(mode * half, T), half)
    share = out.shape[0]

    def load_own(c):
        return pltpu.make_async_copy(tensor.at[:, c, kept], own.at[c], own_sem.at[c])

    def load_theirs(c):
        return pltpu.make_async_copy(arrived.at[c], theirs.at[c], their_sem.at[c])

    def send(c):
        return pltpu.make_async_remote_copy(
            src_ref=slab.at[c, 1],
            dst_ref=out.at[:, c, kept],
            send_sem=send_sem.at[c],
            recv_sem=recv_sem.at[c],
            device_id=other,
        )

    def store(c):
        return pltpu.make_async_copy(slab.at[c, 0], out.at[:, c, kept], store_sem.at[c])

    for c in range(fields):
        load_own(c).start()
        load_theirs(c).start()
    greet(other)

    @pl.loop(0, fields)
    def _(c):
        load_own(c).wait()
        load_theirs(c).wait()
        left = basis[:, pl.ds(pl.multiple_of(mode * rows, T), rows)]
        right = basis[:, pl.ds(pl.multiple_of((1 - mode) * rows, T), rows)]
        both = dot(left, own[c], 1, 0) + dot(right, theirs[c], 1, 0)
        first = mode == 0
        slab[c, 1] = jnp.where(first, both[share:], both[:share])
        send(c).start()
        slab[c, 0] = jnp.where(first, both[:share], both[share:])
        store(c).start()

    for c in range(fields):
        store(c).wait()
        send(c).wait()


def project(basis, tensor, arrived):
    rows, fields, cells = tensor.shape
    share = basis.shape[0] // 2
    any_spec = pl.BlockSpec(memory_space=pl.ANY)
    return pl.pallas_call(
        project_kernel,
        out_shape=jax.ShapeDtypeStruct((share, fields, cells), jnp.float32),
        in_specs=[pl.BlockSpec(memory_space=pltpu.VMEM), any_spec, any_spec],
        out_specs=any_spec,
        scratch_shapes=[
            pltpu.VMEM((fields, rows, cells // 2), jnp.float32),
            pltpu.VMEM((fields, rows, cells // 2), jnp.float32),
            pltpu.VMEM((fields, 2, share, cells // 2), jnp.float32),
        ]
        + [pltpu.SemaphoreType.DMA((fields,))] * 5,
        compiler_params=pltpu.CompilerParams(collective_id=2, has_side_effects=True),
        name="projection",
    )(basis, tensor, arrived)


def local(tensor, start_basis):
    total = tensor.shape[1] * tensor.shape[2] * lax.axis_size("oth")
    diag, cross, arrived = pair(tensor)
    sums = summed(diag, cross).reshape(2, -1, T, T)
    triangle, basis = small(1.0 / total, sums, start_basis)
    return (project(basis, tensor, arrived), triangle)


def solution(mesh):
    return jax.shard_map(
        local,
        mesh=mesh,
        in_specs=(P("mode", None, "oth"), P()),
        out_specs=(P("mode", None, "oth"), P()),
        check_vma=False,
    )
```

```python
import jax
import jax.numpy as jnp
from jax import lax
from jax.experimental import pallas as pl
from jax.experimental.pallas import tpu as pltpu
from jax.sharding import PartitionSpec as P

ITERS = 3
T = 128
XS, YS, ZS = 4, 8, 8
HIGH = lax.Precision.HIGHEST


AXES = {"x": XS, "y": YS, "z": ZS}
CHAINS = ((0, 24, "z", "y"), (192, 24, "y", "z"), (384, 16, "z", "y"), (512, 16, "y", "z"))
PER_CHAIN = 40


def dot(a, b, ca, cb):
    return lax.dot_general(
        a, b, (((ca,), (cb,)), ((), ())), precision=HIGH, preferred_element_type=jnp.float32
    )


def covariance_kernel(
    tensor,
    out,
    field,
    whole,
    got,
    square,
    mixed,
    work,
    cross,
    half_in,
    in1,
    in2,
    in3,
    send_sem,
    recv_sem,
    local_sem,
    given_sem,
    taken_sem,
):
    mode = lax.axis_index("mode")
    oth = lax.axis_index("oth")
    x = lax.rem(oth, XS)
    y = lax.rem(oth // XS, YS)
    z = oth // (XS * YS)
    here = {"x": x, "y": y, "z": z}
    other = {"mode": 1 - mode, "oth": oth}
    fields, rows, cells = whole.shape
    half = cells // 2
    kept = pl.ds(pl.multiple_of(mode * half, T), half)
    away = pl.ds(pl.multiple_of((1 - mode) * half, T), half)
    my_rows = pl.ds(pl.multiple_of(mode * rows, T), rows)
    their_rows = pl.ds(pl.multiple_of((1 - mode) * rows, T), rows)

    def along(axis, place):
        spot = dict(here)
        spot[axis] = place
        return {"mode": mode, "oth": (spot["z"] * YS + spot["y"]) * XS + spot["x"]}

    def peer(axis, step):
        return lax.rem(here[axis] + step, AXES[axis])

    def load(c):
        return pltpu.make_async_copy(tensor.at[:, c, :], whole.at[c], local_sem.at[0, c])

    def keep_own(c):
        return pltpu.make_async_copy(whole.at[c], field.at[c, my_rows, :], local_sem.at[1, c])

    def keep_got(c):
        return pltpu.make_async_copy(got.at[c], field.at[c, their_rows, kept], local_sem.at[2, c])

    def give(c):
        return pltpu.make_async_remote_copy(
            src_ref=whole.at[c, :, away],
            dst_ref=got.at[c],
            send_sem=given_sem.at[0, c],
            recv_sem=taken_sem.at[0, c],
            device_id=other,
        )

    def give_rest(c):
        return pltpu.make_async_remote_copy(
            src_ref=whole.at[c, :, kept],
            dst_ref=field.at[c, my_rows, kept],
            send_sem=given_sem.at[1, c],
            recv_sem=taken_sem.at[1, c],
            device_id=other,
        )

    def copy(src, dst, slot, device):
        return pltpu.make_async_remote_copy(
            src_ref=src,
            dst_ref=dst,
            send_sem=send_sem.at[slot],
            recv_sem=recv_sem.at[slot],
            device_id=device,
        )

    for c in range(fields):
        load(c).start()
    barrier = pltpu.get_barrier_semaphore()
    pl.semaphore_signal(barrier, inc=1, device_id=other)
    count = 1
    for axis in "zyx":
        for step in range(1, AXES[axis]):
            pl.semaphore_signal(barrier, inc=1, device_id=along(axis, peer(axis, step)))
            count += 1
    pl.semaphore_wait(barrier, count)

    used = [0]
    started = []

    def launch(src, dst, device):
        item = copy(src, dst, used[0], device)
        used[0] += 1
        item.start()
        started.append(item)
        return item

    def own_rows(chain):
        base, piece, major, minor = CHAINS[chain]
        return pl.ds(pl.multiple_of(base + here[major] * piece, 8), piece)

    def scatter(chain):
        base, piece, major, minor = CHAINS[chain]
        items = []
        for step in range(1, AXES[major]):
            to = peer(major, step)
            part = pl.ds(pl.multiple_of(base + to * piece, 8), piece)
            spot = in1.at[chain, here[major], pl.ds(0, piece)]
            items.append(launch(work.at[part], spot, along(major, to)))
        in1[chain, here[major], :piece] = work[own_rows(chain)]
        return items

    def total(ref, chain, axis):
        piece = CHAINS[chain][1]
        value = ref[chain, 0, :piece]
        for place in range(1, AXES[axis]):
            value = value + ref[chain, place, :piece]
        return value

    def exchange(chain, value, ref, axis):
        piece = CHAINS[chain][1]
        ref[chain, here[axis], :piece] = value
        spot = ref.at[chain, here[axis], pl.ds(0, piece)]
        return [launch(spot, spot, along(axis, peer(axis, step))) for step in range(1, AXES[axis])]

    def arrive(items):
        for item in items:
            item.wait_recv()

    for c in range(fields):
        load(c).wait()
        give(c).start()
    square[...] = jnp.zeros_like(square)
    mixed[...] = jnp.zeros_like(mixed)

    @pl.loop(0, fields)
    def _(c):
        square[...] += dot(whole[c], whole[c], 1, 1)

    work[:T] = square[:T, :T]
    work[T : 2 * T] = square[T:, :T]
    work[2 * T : 3 * T] = square[T:, T:]
    first = {chain: scatter(chain) for chain in (0, 1)}

    @pl.loop(0, fields)
    def _(c):
        give(c).wait_recv()
        mixed[...] += dot(whole[c, :, kept], got[c], 1, 1)

    lower = jnp.where(mode == 0, mixed[...].T, mixed[...])
    cross[:T] = lower[:T, :T]
    cross[T : 2 * T] = lower[:T, T:]
    cross[2 * T : 3 * T] = lower[T:, :T]
    cross[3 * T :] = lower[T:, T:]
    swap = launch(
        cross.at[pl.ds(pl.multiple_of((1 - mode) * 2 * T, 8), 2 * T)], half_in, other
    )
    swap.wait_recv()
    work[3 * T :] = cross[pl.ds(pl.multiple_of(mode * 2 * T, 8), 2 * T)] + half_in[...]
    first.update({chain: scatter(chain) for chain in (2, 3)})
    for c in range(fields):
        give_rest(c).start()
        keep_own(c).start()
        keep_got(c).start()

    second, third, fourth, passed = {}, {}, {}, []
    for chain, (base, piece, major, minor) in enumerate(CHAINS):
        arrive(first[chain])
        second[chain] = exchange(chain, total(in1, chain, major), in2, minor)
    for chain, (base, piece, major, minor) in enumerate(CHAINS):
        arrive(second[chain])
        third[chain] = exchange(chain, total(in2, chain, minor), in3, "x")
    for chain, (base, piece, major, minor) in enumerate(CHAINS):
        arrive(third[chain])
        out[mode, own_rows(chain)] = total(in3, chain, "x")
        spot = out.at[mode, own_rows(chain)]
        fourth[chain] = [
            launch(spot, spot, along(major, peer(major, step))) for step in range(1, AXES[major])
        ]
        passed.append(launch(spot, spot, other))
    for chain, (base, piece, major, minor) in enumerate(CHAINS):
        for step in range(1, AXES[major]):
            fourth[chain][step - 1].wait_recv()
            source = lax.rem(here[major] + (AXES[major] - step), AXES[major])
            spot = out.at[mode, pl.ds(pl.multiple_of(base + source * piece, 8), piece)]
            passed.append(launch(spot, spot, other))
    arrive(passed)
    for item in started:
        item.wait_send()
    for c in range(fields):
        give(c).wait_send()
        give_rest(c).wait()
        keep_own(c).wait()
        keep_got(c).wait()


def covariance(tensor):
    rows, fields, cells = tensor.shape
    any_spec = pl.BlockSpec(memory_space=pl.ANY)
    vmem = pl.BlockSpec(memory_space=pltpu.VMEM)
    count = len(CHAINS)
    most = max(chain[1] for chain in CHAINS)
    copies = 1 + count * PER_CHAIN
    return pl.pallas_call(
        covariance_kernel,
        out_shape=[
            jax.ShapeDtypeStruct((2, 5 * T, T), jnp.float32),
            jax.ShapeDtypeStruct((fields, 2 * rows, cells), jnp.float32),
        ],
        in_specs=[any_spec],
        out_specs=[vmem, any_spec],
        scratch_shapes=[
            pltpu.VMEM((fields, rows, cells), jnp.float32),
            pltpu.VMEM((fields, rows, cells // 2), jnp.float32),
            pltpu.VMEM((rows, rows), jnp.float32),
            pltpu.VMEM((rows, rows), jnp.float32),
            pltpu.VMEM((5 * T, T), jnp.float32),
            pltpu.VMEM((4 * T, T), jnp.float32),
            pltpu.VMEM((2 * T, T), jnp.float32),
            pltpu.VMEM((count, 8, most, T), jnp.float32),
            pltpu.VMEM((count, 8, most, T), jnp.float32),
            pltpu.VMEM((count, XS, most, T), jnp.float32),
            pltpu.SemaphoreType.DMA((copies,)),
            pltpu.SemaphoreType.DMA((copies,)),
            pltpu.SemaphoreType.DMA((3, fields)),
            pltpu.SemaphoreType.DMA((2, fields)),
            pltpu.SemaphoreType.DMA((2, fields)),
        ],
        compiler_params=pltpu.CompilerParams(collective_id=0, has_side_effects=True),
        name="covariance",
    )(tensor)


def thirds(x):
    high = x.astype(jnp.bfloat16).astype(jnp.float32)
    rest = x - high
    middle = rest.astype(jnp.bfloat16).astype(jnp.float32)
    return high, middle, rest - middle


def outer(a, b):
    ah, am, al = thirds(a)
    bh, bm, bl = thirds(b)
    left = jnp.concatenate([ah, ah, am, am, ah, al], axis=0).astype(jnp.bfloat16)
    right = jnp.concatenate([bh, bm, bh, bm, bl, bh], axis=0).astype(jnp.bfloat16)
    return lax.dot_general(
        left, right, (((0,), (0,)), ((), ())), preferred_element_type=jnp.float32
    )


def factor(mats, uppers):
    groups = T // 8
    lane = lax.broadcasted_iota(jnp.int32, (8, T), 1)
    sub = lax.broadcasted_iota(jnp.int32, (8, T), 0)

    def spread(v, i):
        return jnp.broadcast_to(v[i : i + 1, :], (8, T))

    def column(v, i):
        return jnp.broadcast_to(v[:, i : i + 1], (8, T))

    def body(k, state):
        new_state = []
        keep = lane < jnp.where(k == 0, T, T - 8)
        more = k < groups - 1
        active = (lane >= 8) & (lane < T - 8 * k)
        for (mat, left, right), upper in zip(state, uppers):
            mat = list(mat)
            late = outer(left, right)
            for g in range(1, groups - 1):
                mat[g] = jnp.where(keep, mat[g], 0.0) - late[8 * g : 8 * g + 8, :]
            head, following = mat[0], mat[1]
            heads = [column(head, i) for i in range(8)]
            nexts = [jnp.where(more, column(following, i), 0.0) for i in range(8)]
            done = jnp.zeros((8, T), jnp.float32)
            for i in range(8):
                row = spread(head, i)
                inv = lax.rsqrt(spread(heads[i], i))
                square = inv * inv
                at = lane == i
                row_one = jnp.where(at, 1.0, row)
                scaled = row_one * square
                done = jnp.where(sub == i, row * inv, done)
                below = jnp.where(sub > i, heads[i], 0.0)
                for j in range(i + 1, 8):
                    factor_j = spread(heads[j], i) * square
                    heads[j] = heads[j] - below * factor_j
                    nexts[j] = nexts[j] - nexts[i] * factor_j
                head = jnp.where(at, 0.0, head) - below * scaled
                head = jnp.where(sub == i, row_one * inv, head)
                following = jnp.where(at, 0.0, following) - nexts[i] * scaled
            upper[pl.ds(pl.multiple_of(k * 8, 8), 8), :] = pltpu.roll(done, k * 8, axis=1)
            left = jnp.where(active, head, 0.0)
            right = jnp.where((lane < 8) & (lane > sub), 0.0, head)
            mat = [head, following] + mat[2:]
            mat = [pltpu.roll(m, T - 8, axis=1) for m in mat]
            left = pltpu.roll(left, T - 8, axis=1)
            right = pltpu.roll(right, T - 8, axis=1)
            new_state.append((tuple(mat[1:] + mat[:1]), left, right))
        return tuple(new_state)

    zero = jnp.zeros((8, T), jnp.float32)
    state = tuple(
        (tuple(m[8 * g : 8 * g + 8, :] for g in range(groups)), zero, zero) for m in mats
    )
    state = lax.fori_loop(0, groups, body, state)
    row = lax.broadcasted_iota(jnp.int32, (T, T), 0)
    col = lax.broadcasted_iota(jnp.int32, (T, T), 1)
    inverses = [jnp.where(row >= col, jnp.concatenate(s[0], axis=0), 0.0) for s in state]
    lowers = [jnp.where(row <= col, u[...], 0.0).T for u in uppers]
    return lowers, inverses


PLACES = (((0, 0), (1, 0), (1, 1), (2, 0), (2, 1)), ((2, 2), (3, 2), (3, 3), (3, 0), (3, 1)))


def small_kernel(
    scale, sums, start, triangle, basis_turned, covar, work, images, basis, upper1, upper2
):
    blocks = covar.shape[0] // T
    for m in range(2):
        for b, (r, c) in enumerate(PLACES[m]):
            block = sums[m, b] * scale
            covar[r * T : r * T + T, c * T : c * T + T] = block
            work[r * T : r * T + T, c * T : c * T + T] = block
            if r != c:
                covar[c * T : c * T + T, r * T : r * T + T] = block.T
    basis[...] = start[...]
    for r in range(blocks):
        lo = r * T
        mats = [work[lo : lo + T, lo : lo + T]]
        uppers = [upper1]
        if r < ITERS:
            images[...] = dot(covar[...], basis[...], 1, 0)
            mats.append(dot(images[...], images[...], 0, 0))
            uppers.append(upper2)
        lowers, inverses = factor(mats, uppers)
        triangle[lo : lo + T, lo : lo + T] = lowers[0]
        if r < ITERS - 1:
            basis[...] = dot(images[...], inverses[1], 1, 1)
        elif r == ITERS - 1:
            basis_turned[...] = dot(inverses[1], images[...], 1, 1)
        if r > 0:
            triangle[:lo, lo : lo + T] = jnp.zeros((lo, T), jnp.float32)
        if r < blocks - 1:
            panel = dot(work[lo + T :, lo : lo + T], inverses[0], 1, 1)
            triangle[lo + T :, lo : lo + T] = panel
            for c in range(r + 1, blocks):
                top = c * T
                work[top:, top : top + T] = work[top:, top : top + T] - dot(
                    panel[top - lo - T :, :], panel[top - lo - T : top - lo, :], 1, 1
                )


def small(scale, sums, start_basis):
    n, rank = start_basis.shape
    return pl.pallas_call(
        lambda *refs: small_kernel(scale, *refs),
        out_shape=[
            jax.ShapeDtypeStruct((n, n), jnp.float32),
            jax.ShapeDtypeStruct((rank, n), jnp.float32),
        ],
        in_specs=[pl.BlockSpec(memory_space=pltpu.VMEM)] * 2,
        out_specs=[pl.BlockSpec(memory_space=pltpu.VMEM)] * 2,
        scratch_shapes=[
            pltpu.VMEM((n, n), jnp.float32),
            pltpu.VMEM((n, n), jnp.float32),
            pltpu.VMEM((n, rank), jnp.float32),
            pltpu.VMEM((n, rank), jnp.float32),
            pltpu.VMEM((T, T), jnp.float32),
            pltpu.VMEM((T, T), jnp.float32),
        ],
        name="factors",
    )(sums, start_basis)


def project_kernel(basis, field, out, block, slab, load_sem, store_sem):
    fields, share = slab.shape[:2]
    mine = basis[pl.ds(pl.multiple_of(lax.axis_index("mode") * share, 8), share), :]

    def load(c):
        return pltpu.make_async_copy(field.at[c], block.at[c], load_sem.at[c])

    def store(c):
        return pltpu.make_async_copy(slab.at[c], out.at[:, c, :], store_sem.at[c])

    for c in range(fields):
        load(c).start()
    for c in range(fields):
        load(c).wait()
        slab[c] = dot(mine, block[c], 1, 0)
        store(c).start()
    for c in range(fields):
        store(c).wait()


def project(basis, field):
    fields, rows, cells = field.shape
    share = basis.shape[0] // 2
    any_spec = pl.BlockSpec(memory_space=pl.ANY)
    return pl.pallas_call(
        project_kernel,
        out_shape=jax.ShapeDtypeStruct((share, fields, cells), jnp.float32),
        in_specs=[pl.BlockSpec(memory_space=pltpu.VMEM), any_spec],
        out_specs=any_spec,
        scratch_shapes=[
            pltpu.VMEM((fields, rows, cells), jnp.float32),
            pltpu.VMEM((fields, share, cells), jnp.float32),
            pltpu.SemaphoreType.DMA((fields,)),
            pltpu.SemaphoreType.DMA((fields,)),
        ],
        name="projection",
    )(basis, field)


def local(tensor, start_basis):
    total = tensor.shape[1] * tensor.shape[2] * lax.axis_size("oth")
    sums, field = covariance(tensor)
    triangle, basis = small(1.0 / total, sums.reshape(2, -1, T, T), start_basis)
    return (project(basis, field), triangle)


def solution(mesh):
    return jax.shard_map(
        local,
        mesh=mesh,
        in_specs=(P("mode", None, "oth"), P()),
        out_specs=(P("mode", None, "oth"), P()),
        check_vma=False,
    )
```

```python
import jax
import jax.numpy as jnp
from jax import lax
from jax.experimental import pallas as pl
from jax.experimental.pallas import tpu as pltpu
from jax.sharding import PartitionSpec as P

ITERS = 3
T = 128
XS, YS, ZS = 4, 8, 8
HIGH = lax.Precision.HIGHEST


AXES = {"x": XS, "y": YS, "z": ZS}
CHAINS = ((0, 24, "z", "y"), (192, 24, "y", "z"), (384, 16, "z", "y"), (512, 16, "y", "z"))
PER_CHAIN = 40


def dot(a, b, ca, cb):
    return lax.dot_general(
        a, b, (((ca,), (cb,)), ((), ())), precision=HIGH, preferred_element_type=jnp.float32
    )


def covariance_kernel(
    tensor,
    out,
    field,
    whole,
    got,
    square,
    mixed,
    work,
    cross,
    half_in,
    in1,
    in2,
    in3,
    send_sem,
    recv_sem,
    local_sem,
    given_sem,
    taken_sem,
):
    mode = lax.axis_index("mode")
    oth = lax.axis_index("oth")
    x = lax.rem(oth, XS)
    y = lax.rem(oth // XS, YS)
    z = oth // (XS * YS)
    here = {"x": x, "y": y, "z": z}
    other = {"mode": 1 - mode, "oth": oth}
    fields, rows, cells = whole.shape
    half = cells // 2
    kept = pl.ds(pl.multiple_of(mode * half, T), half)
    away = pl.ds(pl.multiple_of((1 - mode) * half, T), half)
    my_rows = pl.ds(pl.multiple_of(mode * rows, T), rows)
    their_rows = pl.ds(pl.multiple_of((1 - mode) * rows, T), rows)

    def along(axis, place):
        spot = dict(here)
        spot[axis] = place
        return {"mode": mode, "oth": (spot["z"] * YS + spot["y"]) * XS + spot["x"]}

    def peer(axis, step):
        return lax.rem(here[axis] + step, AXES[axis])

    def load(c):
        return pltpu.make_async_copy(tensor.at[:, c, :], whole.at[c], local_sem.at[0, c])

    def keep_own(c):
        return pltpu.make_async_copy(whole.at[c], field.at[c, my_rows, :], local_sem.at[1, c])

    def keep_got(c):
        return pltpu.make_async_copy(got.at[c], field.at[c, their_rows, kept], local_sem.at[2, c])

    def give(c):
        return pltpu.make_async_remote_copy(
            src_ref=whole.at[c, :, away],
            dst_ref=got.at[c],
            send_sem=given_sem.at[0, c],
            recv_sem=taken_sem.at[0, c],
            device_id=other,
        )

    def give_rest(c):
        return pltpu.make_async_remote_copy(
            src_ref=whole.at[c, :, kept],
            dst_ref=field.at[c, my_rows, kept],
            send_sem=given_sem.at[1, c],
            recv_sem=taken_sem.at[1, c],
            device_id=other,
        )

    def copy(src, dst, slot, device):
        return pltpu.make_async_remote_copy(
            src_ref=src,
            dst_ref=dst,
            send_sem=send_sem.at[slot],
            recv_sem=recv_sem.at[slot],
            device_id=device,
        )

    for c in range(fields):
        load(c).start()
    barrier = pltpu.get_barrier_semaphore()
    pl.semaphore_signal(barrier, inc=1, device_id=other)
    count = 1
    for axis in "zyx":
        for step in range(1, AXES[axis]):
            pl.semaphore_signal(barrier, inc=1, device_id=along(axis, peer(axis, step)))
            count += 1
    pl.semaphore_wait(barrier, count)

    used = [0]
    started = []

    def launch(src, dst, device):
        item = copy(src, dst, used[0], device)
        used[0] += 1
        item.start()
        started.append(item)
        return item

    def own_rows(chain):
        base, piece, major, minor = CHAINS[chain]
        return pl.ds(pl.multiple_of(base + here[major] * piece, 8), piece)

    def scatter(chain):
        base, piece, major, minor = CHAINS[chain]
        items = []
        for step in range(1, AXES[major]):
            to = peer(major, step)
            part = pl.ds(pl.multiple_of(base + to * piece, 8), piece)
            spot = in1.at[chain, here[major], pl.ds(0, piece)]
            items.append(launch(work.at[part], spot, along(major, to)))
        in1[chain, here[major], :piece] = work[own_rows(chain)]
        return items

    def total(ref, chain, axis):
        piece = CHAINS[chain][1]
        value = ref[chain, 0, :piece]
        for place in range(1, AXES[axis]):
            value = value + ref[chain, place, :piece]
        return value

    def exchange(chain, value, ref, axis):
        piece = CHAINS[chain][1]
        ref[chain, here[axis], :piece] = value
        spot = ref.at[chain, here[axis], pl.ds(0, piece)]
        return [launch(spot, spot, along(axis, peer(axis, step))) for step in range(1, AXES[axis])]

    def arrive(items):
        for item in items:
            item.wait_recv()

    for c in range(fields):
        load(c).wait()
        give(c).start()
    square[...] = jnp.zeros_like(square)
    mixed[...] = jnp.zeros_like(mixed)

    @pl.loop(0, fields)
    def _(c):
        square[...] += dot(whole[c], whole[c], 1, 1)

    work[:T] = square[:T, :T]
    work[T : 2 * T] = square[T:, :T]
    work[2 * T : 3 * T] = square[T:, T:]
    first = {chain: scatter(chain) for chain in (0, 1)}

    @pl.loop(0, fields)
    def _(c):
        give(c).wait_recv()
        mixed[...] += dot(whole[c, :, kept], got[c], 1, 1)

    lower = jnp.where(mode == 0, mixed[...].T, mixed[...])
    cross[:T] = lower[:T, :T]
    cross[T : 2 * T] = lower[:T, T:]
    cross[2 * T : 3 * T] = lower[T:, :T]
    cross[3 * T :] = lower[T:, T:]
    swap = launch(
        cross.at[pl.ds(pl.multiple_of((1 - mode) * 2 * T, 8), 2 * T)], half_in, other
    )
    swap.wait_recv()
    work[3 * T :] = cross[pl.ds(pl.multiple_of(mode * 2 * T, 8), 2 * T)] + half_in[...]
    first.update({chain: scatter(chain) for chain in (2, 3)})
    for c in range(fields):
        give_rest(c).start()
        keep_own(c).start()
        keep_got(c).start()

    second, third, fourth, passed = {}, {}, {}, []
    for chain, (base, piece, major, minor) in enumerate(CHAINS):
        arrive(first[chain])
        second[chain] = exchange(chain, total(in1, chain, major), in2, minor)
    for chain, (base, piece, major, minor) in enumerate(CHAINS):
        arrive(second[chain])
        third[chain] = exchange(chain, total(in2, chain, minor), in3, "x")
    for chain, (base, piece, major, minor) in enumerate(CHAINS):
        arrive(third[chain])
        out[mode, own_rows(chain)] = total(in3, chain, "x")
        spot = out.at[mode, own_rows(chain)]
        fourth[chain] = [
            launch(spot, spot, along(major, peer(major, step))) for step in range(1, AXES[major])
        ]
        passed.append(launch(spot, spot, other))
    for chain, (base, piece, major, minor) in enumerate(CHAINS):
        for step in range(1, AXES[major]):
            fourth[chain][step - 1].wait_recv()
            source = lax.rem(here[major] + (AXES[major] - step), AXES[major])
            spot = out.at[mode, pl.ds(pl.multiple_of(base + source * piece, 8), piece)]
            passed.append(launch(spot, spot, other))
    arrive(passed)
    for item in started:
        item.wait_send()
    for c in range(fields):
        give(c).wait_send()
        give_rest(c).wait()
        keep_own(c).wait()
        keep_got(c).wait()


def covariance(tensor):
    rows, fields, cells = tensor.shape
    any_spec = pl.BlockSpec(memory_space=pl.ANY)
    vmem = pl.BlockSpec(memory_space=pltpu.VMEM)
    count = len(CHAINS)
    most = max(chain[1] for chain in CHAINS)
    copies = 1 + count * PER_CHAIN
    return pl.pallas_call(
        covariance_kernel,
        out_shape=[
            jax.ShapeDtypeStruct((2, 5 * T, T), jnp.float32),
            jax.ShapeDtypeStruct((fields, 2 * rows, cells), jnp.float32),
        ],
        in_specs=[any_spec],
        out_specs=[vmem, any_spec],
        scratch_shapes=[
            pltpu.VMEM((fields, rows, cells), jnp.float32),
            pltpu.VMEM((fields, rows, cells // 2), jnp.float32),
            pltpu.VMEM((rows, rows), jnp.float32),
            pltpu.VMEM((rows, rows), jnp.float32),
            pltpu.VMEM((5 * T, T), jnp.float32),
            pltpu.VMEM((4 * T, T), jnp.float32),
            pltpu.VMEM((2 * T, T), jnp.float32),
            pltpu.VMEM((count, 8, most, T), jnp.float32),
            pltpu.VMEM((count, 8, most, T), jnp.float32),
            pltpu.VMEM((count, XS, most, T), jnp.float32),
            pltpu.SemaphoreType.DMA((copies,)),
            pltpu.SemaphoreType.DMA((copies,)),
            pltpu.SemaphoreType.DMA((3, fields)),
            pltpu.SemaphoreType.DMA((2, fields)),
            pltpu.SemaphoreType.DMA((2, fields)),
        ],
        compiler_params=pltpu.CompilerParams(collective_id=0, has_side_effects=True),
        name="covariance",
    )(tensor)


def thirds(x):
    high = x.astype(jnp.bfloat16).astype(jnp.float32)
    rest = x - high
    middle = rest.astype(jnp.bfloat16).astype(jnp.float32)
    return high, middle, rest - middle


def outer(a, b):
    ah, am, al = thirds(a)
    bh, bm, bl = thirds(b)
    left = jnp.concatenate([ah, ah, am, am, ah, al], axis=0).astype(jnp.bfloat16)
    right = jnp.concatenate([bh, bm, bh, bm, bl, bh], axis=0).astype(jnp.bfloat16)
    return lax.dot_general(
        left, right, (((0,), (0,)), ((), ())), preferred_element_type=jnp.float32
    )


def factor(mats, uppers):
    groups = T // 8
    lane = lax.broadcasted_iota(jnp.int32, (8, T), 1)
    sub = lax.broadcasted_iota(jnp.int32, (8, T), 0)

    def spread(v, i):
        return jnp.broadcast_to(v[i : i + 1, :], (8, T))

    def column(v, i):
        return jnp.broadcast_to(v[:, i : i + 1], (8, T))

    states = [[[m[8 * g : 8 * g + 8, :] for g in range(groups)], None, None] for m in mats]
    for k in range(groups):
        first = 8 * k
        for state, upper in zip(states, uppers):
            mat, left, right = state
            if k > 0:
                late = outer(left, right)
                before = (lane >= first - 8) & (lane < first)
                for g in range(k + 1, groups):
                    mat[g] = jnp.where(before, 0.0, mat[g]) - late[8 * g : 8 * g + 8, :]
            last = k == groups - 1
            head = mat[k]
            heads = [column(head, first + i) for i in range(8)]
            if not last:
                following = mat[k + 1]
                nexts = [column(following, first + i) for i in range(8)]
            done = jnp.zeros((8, T), jnp.float32)
            for i in range(8):
                row = spread(head, i)
                inv = lax.rsqrt(spread(heads[i], i))
                square = inv * inv
                at = lane == first + i
                row_one = jnp.where(at, 1.0, row)
                scaled = row_one * square
                done = jnp.where(sub == i, row * inv, done)
                below = jnp.where(sub > i, heads[i], 0.0)
                for j in range(i + 1, 8):
                    entry = spread(heads[j], i)
                    heads[j] = heads[j] - (below * entry) * square
                    if not last:
                        nexts[j] = nexts[j] - nexts[i] * (entry * square)
                head = jnp.where(at, 0.0, head) - below * scaled
                head = jnp.where(sub == i, row_one * inv, head)
                if not last:
                    following = jnp.where(at, 0.0, following) - nexts[i] * scaled
            upper[first : first + 8, :] = done
            state[1] = jnp.where(lane >= first + 8, head, 0.0)
            inside = (lane >= first) & (lane < first + 8) & (lane - first > sub)
            state[2] = jnp.where(inside, 0.0, head)
            mat[k] = head
            if not last:
                mat[k + 1] = following
    row = lax.broadcasted_iota(jnp.int32, (T, T), 0)
    col = lax.broadcasted_iota(jnp.int32, (T, T), 1)
    inverses = [jnp.where(row >= col, jnp.concatenate(s[0], axis=0), 0.0) for s in states]
    lowers = [jnp.where(row <= col, u[...], 0.0).T for u in uppers]
    return lowers, inverses


PLACES = (((0, 0), (1, 0), (1, 1), (2, 0), (2, 1)), ((2, 2), (3, 2), (3, 3), (3, 0), (3, 1)))


def small_kernel(
    scale, sums, start, triangle, basis_turned, covar, work, images, basis, upper1, upper2
):
    blocks = covar.shape[0] // T
    for m in range(2):
        for b, (r, c) in enumerate(PLACES[m]):
            block = sums[m, b] * scale
            covar[r * T : r * T + T, c * T : c * T + T] = block
            work[r * T : r * T + T, c * T : c * T + T] = block
            if r != c:
                covar[c * T : c * T + T, r * T : r * T + T] = block.T
    basis[...] = start[...]
    for r in range(blocks):
        lo = r * T
        mats = [work[lo : lo + T, lo : lo + T]]
        uppers = [upper1]
        if r < ITERS:
            images[...] = dot(covar[...], basis[...], 1, 0)
            mats.append(dot(images[...], images[...], 0, 0))
            uppers.append(upper2)
        lowers, inverses = factor(mats, uppers)
        triangle[lo : lo + T, lo : lo + T] = lowers[0]
        if r < ITERS - 1:
            basis[...] = dot(images[...], inverses[1], 1, 1)
        elif r == ITERS - 1:
            basis_turned[...] = dot(inverses[1], images[...], 1, 1)
        if r > 0:
            triangle[:lo, lo : lo + T] = jnp.zeros((lo, T), jnp.float32)
        if r < blocks - 1:
            panel = dot(work[lo + T :, lo : lo + T], inverses[0], 1, 1)
            triangle[lo + T :, lo : lo + T] = panel
            for c in range(r + 1, blocks):
                top = c * T
                work[top:, top : top + T] = work[top:, top : top + T] - dot(
                    panel[top - lo - T :, :], panel[top - lo - T : top - lo, :], 1, 1
                )


def small(scale, sums, start_basis):
    n, rank = start_basis.shape
    return pl.pallas_call(
        lambda *refs: small_kernel(scale, *refs),
        out_shape=[
            jax.ShapeDtypeStruct((n, n), jnp.float32),
            jax.ShapeDtypeStruct((rank, n), jnp.float32),
        ],
        in_specs=[pl.BlockSpec(memory_space=pltpu.VMEM)] * 2,
        out_specs=[pl.BlockSpec(memory_space=pltpu.VMEM)] * 2,
        scratch_shapes=[
            pltpu.VMEM((n, n), jnp.float32),
            pltpu.VMEM((n, n), jnp.float32),
            pltpu.VMEM((n, rank), jnp.float32),
            pltpu.VMEM((n, rank), jnp.float32),
            pltpu.VMEM((T, T), jnp.float32),
            pltpu.VMEM((T, T), jnp.float32),
        ],
        name="factors",
    )(sums, start_basis)


def project_kernel(basis, field, out, block, slab, load_sem, store_sem):
    fields, share = slab.shape[:2]
    mine = basis[pl.ds(pl.multiple_of(lax.axis_index("mode") * share, 8), share), :]

    def load(c):
        return pltpu.make_async_copy(field.at[c], block.at[c], load_sem.at[c])

    def store(c):
        return pltpu.make_async_copy(slab.at[c], out.at[:, c, :], store_sem.at[c])

    for c in range(fields):
        load(c).start()
    high = mine.astype(jnp.bfloat16)
    low = (mine - high.astype(jnp.float32)).astype(jnp.bfloat16)
    stacked = jnp.concatenate([high, low], axis=0)
    for c in range(fields):
        load(c).wait()
        values = block[c]
        main = values.astype(jnp.bfloat16)
        rest = (values - main.astype(jnp.float32)).astype(jnp.bfloat16)
        wide = jnp.dot(stacked, main, preferred_element_type=jnp.float32)
        thin = jnp.dot(high, rest, preferred_element_type=jnp.float32)
        slab[c] = wide[:share] + (wide[share:] + thin)
        store(c).start()
    for c in range(fields):
        store(c).wait()


def project(basis, field):
    fields, rows, cells = field.shape
    share = basis.shape[0] // 2
    any_spec = pl.BlockSpec(memory_space=pl.ANY)
    return pl.pallas_call(
        project_kernel,
        out_shape=jax.ShapeDtypeStruct((share, fields, cells), jnp.float32),
        in_specs=[pl.BlockSpec(memory_space=pltpu.VMEM), any_spec],
        out_specs=any_spec,
        scratch_shapes=[
            pltpu.VMEM((fields, rows, cells), jnp.float32),
            pltpu.VMEM((fields, share, cells), jnp.float32),
            pltpu.SemaphoreType.DMA((fields,)),
            pltpu.SemaphoreType.DMA((fields,)),
        ],
        name="projection",
    )(basis, field)


def local(tensor, start_basis):
    total = tensor.shape[1] * tensor.shape[2] * lax.axis_size("oth")
    sums, field = covariance(tensor)
    triangle, basis = small(1.0 / total, sums.reshape(2, -1, T, T), start_basis)
    return (project(basis, field), triangle)


def solution(mesh):
    return jax.shard_map(
        local,
        mesh=mesh,
        in_specs=(P("mode", None, "oth"), P()),
        out_specs=(P("mode", None, "oth"), P()),
        check_vma=False,
    )
```
